128 devices in a mesh: dp: 16 (over y, z_hi, core), fsdp: 8 (over z_lo, x).
Axes of the slice: x: 4, y: 4, z: 4 (z_hi: 2, z_lo: 2; z = z_hi * 2 + z_lo), core: 2. Of those that a mesh axis runs over, the one named last changes fastest.
Arguments:
- pooled: bfloat16 [16384, 256, 128], P(None, ('dp', 'fsdp')), may hold values from -6 to 6
- feature_order: int32 [256], replicated, may hold values from 0 to 255, each once
- fm_proj: bfloat16 [2, 256, 16], replicated, may hold values from -0.375 to 0.375
- fm_gain: float32 [2, 4096], replicated, may hold values from 0.1 to 1.9
- mlp_weight: bfloat16 [2, 4096, 2048], P(None, None, 'fsdp'), may hold values from -0.09375 to 0.09375
- lcb_weight: bfloat16 [2, 240, 256], replicated, may hold values from -0.375 to 0.375
- out_gain: float32 [2, 128], replicated, may hold values from 0.1 to 1.9
Outputs:
- layer_out: bfloat16 [16384, 256, 128], P(('dp', 'fsdp'))
The draws below stay inside these ranges and needn't reach their ends.
Inputs may be any that keep to these rules, and one draw needn't show every extreme that they name: feature_order names every feature exactly once.
All inputs are finite; a program needn't handle non-finite values.
Results may differ from the reference program's by a relative error of at most 0.0051.
Values may be sent and summed in bfloat16 or wider, within the bound.
A program may use at most 192 MiB of HBM per device.

```python
import math
import jax
import jax.numpy as jnp
from jax import lax

N = 256
D = 128
K = 16
NF = 16
LAYERS = 2
FLAT = 4096
NL = 240
SAMPLES = 16384


def steps_of(stream_key, shape, split, low, largest):
    factor_of = 1.0
    for axis_at, shards_of in split:
        draws = jax.random.uniform(jax.random.fold_in(jax.random.fold_in(stream_key, 6), axis_at), (shards_of,), jnp.float32, low / len(split), largest / len(split))
        factor_of = factor_of * jnp.repeat(jnp.exp(draws), shape[axis_at] // shards_of).reshape((-1,) + (1,) * (len(shape) - 1 - axis_at))
    return factor_of


def normal_values(rng, dims, scale, bound, shards=(), dtype=jnp.bfloat16):
    entries = jax.random.normal(rng, dims, jnp.float32) * scale
    if len(shards) > 0:
        entries = steps_of(rng, dims, shards, -0.22, 0.18) * entries
    return jnp.clip(entries, min=-bound, max=bound).astype(dtype)


def setup_inputs(seed: int = 0) -> dict:
    arg_keys = jax.random.split(jax.random.key(seed), 8)
    pooled = normal_values(arg_keys[0], (SAMPLES, N, D), 1.0, 6.0, ((1, 128),))
    feature_order = jax.random.permutation(arg_keys[1], N).astype(jnp.int32)
    fm_proj = normal_values(arg_keys[2], (LAYERS, N, K), N ** -0.5, 0.375)
    fm_gain = jnp.clip(1.0 + 0.18 * jax.random.normal(arg_keys[3], (LAYERS, FLAT), jnp.float32), 0.1, 1.9)
    mlp_weight = normal_values(arg_keys[4], (LAYERS, FLAT, NF * D), FLAT ** -0.5, 0.09375, ((2, 8),))
    lcb_weight = normal_values(arg_keys[5], (LAYERS, NL, N), N ** -0.5, 0.375)
    out_gain = jnp.clip(1.0 + 0.18 * jax.random.normal(arg_keys[6], (LAYERS, D), jnp.float32), 0.1, 1.9)
    return dict(pooled=pooled, feature_order=feature_order, fm_proj=fm_proj, fm_gain=fm_gain, mlp_weight=mlp_weight, lcb_weight=lcb_weight, out_gain=out_gain)


def interaction_layer(features, proj_mat, gain_flat, mlp_mat, lcb_mat, gain_out):
    block_rows = features.shape[0]
    features_f32 = features.astype(jnp.float32)
    projected = jnp.einsum('bnd,nk->bdk', features_f32, proj_mat.astype(jnp.float32)).astype(jnp.bfloat16)
    interaction = jnp.einsum('bnd,bdk->bnk', features_f32, projected.astype(jnp.float32))
    flattened = interaction.reshape(block_rows, N * K)
    center = lax.optimization_barrier(jnp.mean(flattened, axis=-1, keepdims=True))
    spread = lax.optimization_barrier(jnp.mean((flattened - center) ** 2, axis=-1, keepdims=True))
    normed = ((flattened - center) * lax.rsqrt(spread + 1e-05) * gain_flat).astype(jnp.bfloat16)
    fm_out = jnp.dot(normed, mlp_mat, preferred_element_type=jnp.float32).astype(jnp.bfloat16)
    fm_out = fm_out.reshape(block_rows, NF, D)
    lcb_out = jnp.einsum('ln,bnd->bld', lcb_mat.astype(jnp.float32), features_f32)
    combined = jnp.concatenate([fm_out.astype(jnp.float32), lcb_out], axis=1) + features_f32
    mid = lax.optimization_barrier(jnp.mean(combined, axis=-1, keepdims=True))
    width_var = lax.optimization_barrier(jnp.mean((combined - mid) ** 2, axis=-1, keepdims=True))
    return ((combined - mid) * lax.rsqrt(width_var + 1e-05) * gain_out).astype(jnp.bfloat16)

def reference(pooled, feature_order, fm_proj, fm_gain, mlp_weight, lcb_weight, out_gain):
    slot_of = jnp.argsort(feature_order).astype(jnp.int32)
    block_size = math.gcd(SAMPLES, 128)
    blocks = pooled.reshape(SAMPLES // block_size, block_size, N, D)

    def run_block(block):
        features = jnp.take(block, slot_of, axis=1)
        for layer_index in range(LAYERS):
            features = interaction_layer(features, fm_proj[layer_index], fm_gain[layer_index], mlp_weight[layer_index], lcb_weight[layer_index], out_gain[layer_index])
        return features
    return lax.map(run_block, blocks).reshape(SAMPLES, N, D)
```

```python
import jax
import jax.numpy as jnp
from jax import lax
from jax.experimental import pallas as pl
from jax.experimental.pallas import tpu as pltpu
from jax.sharding import PartitionSpec as P

N = 256
D = 128
K = 16
LAYERS = 2
DEVICES = 128
BLOCK = 128
CHUNKS = 4
STEP = BLOCK // CHUNKS
HALF = K // 2
MESH = pl.DeviceIdType.MESH
F32 = jnp.float32
BF16 = jnp.bfloat16


def position():
    dp, fsdp = lax.axis_index("dp"), lax.axis_index("fsdp")
    y, z_hi, core = dp // 4, lax.rem(dp // 2, 2), lax.rem(dp, 2)
    z_lo, x = fsdp // 4, lax.rem(fsdp, 4)
    return x, y, z_hi * 2 + z_lo, core


def device_at(x, y, z, core):
    x, y, z = lax.rem(x + 4, 4), lax.rem(y + 4, 4), lax.rem(z + 4, 4)
    return {"dp": (y * 2 + z // 2) * 2 + core, "fsdp": lax.rem(z, 2) * 4 + x}


def gather_kernel(rows, shard, out, full, send, arrive, w_send, w_arrive, own, w_own):
    dp, fsdp = lax.axis_index("dp"), lax.axis_index("fsdp")
    me = dp * 8 + fsdp
    x, y, z, core = position()
    z_lo = lax.rem(z, 2)
    barrier = pltpu.get_barrier_semaphore()

    def mesh_of(t):
        return {"dp": t // 8, "fsdp": lax.rem(t, 8)}

    def greet(i, carry):
        pl.semaphore_signal(
            barrier, inc=1, device_id=mesh_of(lax.rem(me + i, DEVICES)), device_id_type=MESH
        )
        return carry

    lax.fori_loop(1, DEVICES, greet, 0)

    base = core * HALF
    mine = base + 4 + y

    def cols(i):
        return pl.ds(pl.multiple_of(i * 256, 256), 256)

    own_copies = []
    for layer in range(LAYERS):
        for j, (first, count) in enumerate(((base, 4), (mine, 1))):
            copy = pltpu.make_async_copy(
                shard.at[layer, pl.ds(first, count)],
                full.at[layer, pl.ds(first, count), :, cols(fsdp)],
                w_own.at[layer, j],
            )
            copy.start()
            own_copies.append(copy)
    pl.semaphore_wait(barrier, DEVICES - 1)

    def push(layer, slot, source, target, device):
        copy = pltpu.make_async_remote_copy(
            src_ref=source,
            dst_ref=target,
            send_sem=w_send.at[layer, slot],
            recv_sem=w_arrive.at[layer, slot],
            device_id=device,
            device_id_type=MESH,
        )
        copy.start()
        return copy

    right = device_at(x + 1, y, z, core)
    left = device_at(x - 1, y, z, core)
    z_up = device_at(x, y, z + 1, core)
    z_down = device_at(x, y, z - 1, core)
    y_up = device_at(x, y + 1, z, core)
    y_down = device_at(x, y - 1, z, core)
    sibling = device_at(x, y, z, 1 - core)
    from_left = z_lo * 4 + lax.rem(x + 3, 4)
    from_right = z_lo * 4 + lax.rem(x + 1, 4)
    top, bottom = pl.ds(0, 128), pl.ds(128, 128)
    started = []

    def x_first(layer):
        many, one = pl.ds(base, 4), pl.ds(mine, 1)
        return [
            push(layer, 0, shard.at[layer, many], full.at[layer, many, :, cols(fsdp)], right),
            push(layer, 1, shard.at[layer, many], full.at[layer, many, :, cols(fsdp)], left),
            push(layer, 2, shard.at[layer, one], full.at[layer, one, :, cols(fsdp)], right),
            push(layer, 3, shard.at[layer, one], full.at[layer, one, :, cols(fsdp)], left),
        ]

    def same(layer, slot, block, device):
        return push(layer, slot, block, block, device)

    def x_second(layer):
        low, high = pl.ds(base, 2), pl.ds(base + 2, 2)
        return [
            same(layer, 4, full.at[layer, low, :, cols(from_left)], right),
            same(layer, 5, full.at[layer, high, :, cols(from_right)], left),
            same(layer, 6, full.at[layer, mine, top, cols(from_left)], right),
            same(layer, 7, full.at[layer, mine, bottom, cols(from_right)], left),
        ]

    def z_step(layer):
        low, high = pl.ds(base, 2), pl.ds(base + 2, 2)
        group = pl.ds(pl.multiple_of(z_lo * 1024, 1024), 1024)
        return [
            same(layer, 8, full.at[layer, low, :, group], z_up),
            same(layer, 9, full.at[layer, high, :, group], z_down),
            same(layer, 10, full.at[layer, mine, top, group], z_up),
            same(layer, 11, full.at[layer, mine, bottom, group], z_down),
        ]

    def y_first(layer):
        four = pl.ds(base, 4)
        return [
            same(layer, 12, full.at[layer, mine], y_up),
            same(layer, 13, full.at[layer, mine], y_down),
            same(layer, 14, full.at[layer, four], sibling),
        ]

    def y_second(layer):
        lower = base + 4 + lax.rem(y + 3, 4)
        upper = base + 4 + lax.rem(y + 1, 4)
        return [
            same(layer, 15, full.at[layer, lower, top], y_up),
            same(layer, 16, full.at[layer, upper, bottom], y_down),
        ]

    def across(layer):
        return [same(layer, 17, full.at[layer, pl.ds(base + 4, 4)], sibling)]

    def exchange(c):
        def send_one(i, carry):
            t = lax.rem(me + i, DEVICES)
            pltpu.make_async_remote_copy(
                src_ref=rows.at[pl.ds(t * BLOCK + c * STEP, STEP)],
                dst_ref=out.at[pl.ds(c * STEP, STEP), pl.ds(pl.multiple_of(2 * me, 2), 2)],
                send_sem=send.at[c],
                recv_sem=arrive.at[c],
                device_id=mesh_of(t),
                device_id_type=MESH,
            ).start()
            return carry

        lax.fori_loop(1, DEVICES, send_one, 0)
        pltpu.make_async_copy(
            rows.at[pl.ds(me * BLOCK + c * STEP, STEP)],
            out.at[pl.ds(c * STEP, STEP), pl.ds(pl.multiple_of(2 * me, 2), 2)],
            own.at[c],
        ).start()

    def arrived(copies):
        for copy in copies:
            copy.wait_recv()

    first = [x_first(0), x_first(1)]
    exchange(0)
    for copy in own_copies:
        copy.wait()
    second = []
    for layer in range(LAYERS):
        arrived(first[layer])
        second.append(x_second(layer))
    exchange(1)
    third = []
    for layer in range(LAYERS):
        arrived(second[layer])
        third.append(z_step(layer))
    exchange(2)
    fourth = []
    for layer in range(LAYERS):
        arrived(third[layer])
        fourth.append(y_first(layer))
    exchange(3)
    fifth = []
    for layer in range(LAYERS):
        arrived(fourth[layer])
        fifth.append(y_second(layer))
    sixth = []
    for layer in range(LAYERS):
        arrived(fifth[layer])
        sixth.append(across(layer))
    for layer in range(LAYERS):
        arrived(sixth[layer])
    for group in first + second + third + fourth + fifth + sixth:
        for copy in group:
            copy.wait_send()

    for c in range(CHUNKS):
        pltpu.make_async_copy(
            rows.at[pl.ds(0, STEP)], out.at[pl.ds(c * STEP, STEP), pl.ds(0, 2)], own.at[c]
        ).wait()
        part = out.at[pl.ds(c * STEP, STEP), pl.ds(0, N - 2)]
        pltpu.make_async_copy(part, part, arrive.at[c]).wait()
        pltpu.make_async_copy(part, part, send.at[c]).wait()


def gather(rows, shard):
    slots = 18
    return pl.pallas_call(
        gather_kernel,
        out_shape=(
            jax.ShapeDtypeStruct((BLOCK, N, D), BF16),
            jax.ShapeDtypeStruct((LAYERS, K, N, 2048), BF16),
        ),
        in_specs=[pl.BlockSpec(memory_space=pl.ANY)] * 2,
        out_specs=[pl.BlockSpec(memory_space=pl.ANY)] * 2,
        scratch_shapes=[
            pltpu.SemaphoreType.DMA((CHUNKS,)),
            pltpu.SemaphoreType.DMA((CHUNKS,)),
            pltpu.SemaphoreType.DMA((LAYERS, slots)),
            pltpu.SemaphoreType.DMA((LAYERS, slots)),
            pltpu.SemaphoreType.DMA((CHUNKS,)),
            pltpu.SemaphoreType.DMA((LAYERS, 2)),
        ],
        compiler_params=pltpu.CompilerParams(collective_id=0, has_side_effects=True),
    )(rows, shard)


def normalized(values, gain):
    center = jnp.mean(values, axis=-1, keepdims=True)
    apart = values - center
    spread = jnp.mean(apart * apart, axis=-1, keepdims=True)
    return (apart * lax.rsqrt(spread + 1e-05) * gain).astype(BF16)


def features_of_block(count, block, order, weights, layer, mixer, gains, out_gain, inter, fm):
    def pair(i, carry):
        a, b = 2 * i, 2 * i + 1
        both = jnp.concatenate([block[a], block[b]], axis=1)
        if order is not None:
            both = jnp.dot(order, both, preferred_element_type=F32).astype(BF16)
        mixed = jnp.dot(mixer[layer], both, preferred_element_type=F32)
        projected = mixed[:K].astype(BF16)
        for s, at in ((a, 0), (b, D)):
            rows = both[:, at : at + D]
            products = lax.dot_general(
                projected[:, at : at + D],
                rows,
                (((1,), (1,)), ((), ())),
                preferred_element_type=F32,
            )
            for half in range(2):
                inter[half, pl.ds(pl.multiple_of(s * K, K), K), :] = products[
                    :, half * D : (half + 1) * D
                ]
            combined = mixed[K:, at : at + D] + rows[K:].astype(F32)
            block[s, :K] = rows[:K]
            block[s, K:] = normalized(combined, out_gain[layer])
        return carry

    lax.fori_loop(0, count // 2, pair, 0)

    def taken(k):
        return jnp.concatenate(
            [inter[half, pl.ds(k, count, stride=K), :] for half in range(2)], axis=1
        )

    total = jnp.zeros((count, N), F32)
    for k in range(K):
        total += taken(k)
    center = jnp.sum(total, axis=-1, keepdims=True) * (1.0 / (N * K))
    squares = jnp.zeros((count, N), F32)
    for k in range(K):
        apart = taken(k) - center
        squares += apart * apart
    scale = lax.rsqrt(jnp.sum(squares, axis=-1, keepdims=True) * (1.0 / (N * K)) + 1e-05)
    width = 512

    def columns(j, carry):
        at = pl.multiple_of(j * width, width)
        made = jnp.zeros((count, width), F32)
        for k in range(K):
            apart = taken(k) - center
            normed = (apart * scale * gains[layer, k : k + 1, :]).astype(BF16)
            made += jnp.dot(
                normed, weights[layer, k, :, pl.ds(at, width)], preferred_element_type=F32
            )
        made = made.astype(BF16).astype(F32)
        for f in range(width // D):
            fm[pl.ds(j * (width // D) + f, count, stride=K), :] = made[:, f * D : (f + 1) * D]
        return carry

    lax.fori_loop(0, 2048 // width, columns, 0)

    def finish(s, carry):
        combined = fm[pl.ds(pl.multiple_of(s * K, K), K), :] + block[s, :K].astype(F32)
        block[s, :K] = normalized(combined, out_gain[layer])
        return carry

    lax.fori_loop(0, count, finish, 0)


def layers_kernel(x, full, slots, mixer, gains, out_gain, out, block, weights, inter, fm, sem):
    take = pltpu.make_async_copy(x, block, sem.at[0])
    take.start()
    loads = []
    for layer in range(LAYERS):
        load = pltpu.make_async_copy(full.at[layer], weights.at[layer], sem.at[1 + layer])
        load.start()
        loads.append(load)
    order = jnp.where(
        lax.broadcasted_iota(jnp.int32, (N, N), 0) == slots[...], 1.0, 0.0
    ).astype(BF16)
    take.wait()
    for layer in range(LAYERS):
        loads[layer].wait()
        features_of_block(
            BLOCK,
            block,
            order if layer == 0 else None,
            weights,
            layer,
            mixer,
            gains,
            out_gain,
            inter,
            fm,
        )
    give = pltpu.make_async_copy(block, out, sem.at[0])
    give.start()
    give.wait()


def layers(x, full, slots, mixer, gains, out_gain):
    vmem = pl.BlockSpec(memory_space=pltpu.VMEM)
    hbm = pl.BlockSpec(memory_space=pl.ANY)
    return pl.pallas_call(
        layers_kernel,
        out_shape=jax.ShapeDtypeStruct((BLOCK, N, D), BF16),
        in_specs=[hbm, hbm, vmem, vmem, vmem, vmem],
        out_specs=hbm,
        scratch_shapes=[
            pltpu.VMEM((BLOCK, N, D), BF16),
            pltpu.VMEM((LAYERS, K, N, 2048), BF16),
            pltpu.VMEM((2, BLOCK * K, D), F32),
            pltpu.VMEM((BLOCK * K, D), F32),
            pltpu.SemaphoreType.DMA((3,)),
        ],
        compiler_params=pltpu.CompilerParams(vmem_limit_bytes=60 << 20),
    )(x, full, slots, mixer, gains, out_gain)


def body(pooled, feature_order, fm_proj, fm_gain, mlp_weight, lcb_weight, out_gain):
    shard = mlp_weight.reshape(LAYERS, N, K, 256).transpose(0, 2, 1, 3)
    gains = fm_gain.reshape(LAYERS, N, K).transpose(0, 2, 1)
    mixer = jnp.concatenate([fm_proj.transpose(0, 2, 1), lcb_weight], axis=1)
    x, full = gather(pooled, shard)
    return layers(
        x, full, feature_order.reshape(1, N), mixer, gains, out_gain.reshape(LAYERS, 1, D)
    )


def solution(mesh):
    placed = (P(None, ("dp", "fsdp"), None), P(), P(), P(), P(None, None, "fsdp"), P(), P())
    return jax.shard_map(
        body, mesh=mesh, in_specs=placed, out_specs=P(("dp", "fsdp"), None, None), check_vma=False
    )
```

```python
import jax
import jax.numpy as jnp
from jax import lax
from jax.experimental import pallas as pl
from jax.experimental.pallas import tpu as pltpu
from jax.sharding import PartitionSpec as P

N = 256
D = 128
K = 16
LAYERS = 2
DEVICES = 128
BLOCK = 128
CHUNKS = 4
STEP = BLOCK // CHUNKS
HALF = K // 2
MESH = pl.DeviceIdType.MESH
F32 = jnp.float32
BF16 = jnp.bfloat16


def position():
    dp, fsdp = lax.axis_index("dp"), lax.axis_index("fsdp")
    y, z_hi, core = dp // 4, lax.rem(dp // 2, 2), lax.rem(dp, 2)
    z_lo, x = fsdp // 4, lax.rem(fsdp, 4)
    return x, y, z_hi * 2 + z_lo, core


def device_at(x, y, z, core):
    x, y, z = lax.rem(x + 4, 4), lax.rem(y + 4, 4), lax.rem(z + 4, 4)
    return {"dp": (y * 2 + z // 2) * 2 + core, "fsdp": lax.rem(z, 2) * 4 + x}


def normalized(values, gain):
    center = jnp.mean(values, axis=-1, keepdims=True)
    apart = values - center
    spread = jnp.mean(apart * apart, axis=-1, keepdims=True)
    return (apart * lax.rsqrt(spread + 1e-05) * gain).astype(BF16)


def features_of_block(start, count, block, order, weights, layer, mixer, gains, out_gain, inter, fm):
    def pair(i, carry):
        a = start + 2 * i
        both = jnp.concatenate([block[a], block[a + 1]], axis=1)
        if order is not None:
            both = jnp.dot(order[...], both, preferred_element_type=F32).astype(BF16)
        mixed = jnp.dot(mixer[layer], both, preferred_element_type=F32)
        projected = mixed[:K].astype(BF16)
        none = jnp.zeros((K, D), BF16)
        apart = jnp.concatenate(
            [
                jnp.concatenate([projected[:, :D], none], axis=1),
                jnp.concatenate([none, projected[:, D:]], axis=1),
            ],
            axis=0,
        )
        products = lax.dot_general(
            apart, both, (((1,), (1,)), ((), ())), preferred_element_type=F32
        )
        for half in range(2):
            inter[half, pl.ds(pl.multiple_of(2 * i * K, 2 * K), 2 * K), :] = products[
                :, half * D : (half + 1) * D
            ]
        for s, at in ((a, 0), (a + 1, D)):
            rows = both[:, at : at + D]
            combined = mixed[K:, at : at + D] + rows[K:].astype(F32)
            block[s, :K] = rows[:K]
            block[s, K:] = normalized(combined, out_gain[layer])
        return carry

    lax.fori_loop(0, count // 2, pair, 0, unroll=8)

    def taken(k):
        return jnp.concatenate(
            [inter[half, pl.ds(k, count, stride=K), :] for half in range(2)], axis=1
        )

    total = jnp.zeros((count, N), F32)
    for k in range(K):
        total += taken(k)
    center = jnp.sum(total, axis=-1, keepdims=True) * (1.0 / (N * K))
    squares = jnp.zeros((count, N), F32)
    for k in range(K):
        apart = taken(k) - center
        squares += apart * apart
    scale = lax.rsqrt(jnp.sum(squares, axis=-1, keepdims=True) * (1.0 / (N * K)) + 1e-05)
    width = 1024

    def columns(j, carry):
        at = pl.multiple_of(j * width, width)
        made = jnp.zeros((count, width), F32)
        for k in range(K):
            apart = taken(k) - center
            normed = (apart * scale * gains[layer, k : k + 1, :]).astype(BF16)
            made += jnp.dot(
                normed, weights[layer, k, :, pl.ds(at, width)], preferred_element_type=F32
            )
        made = made.astype(BF16).astype(F32)
        for f in range(width // D):
            fm[pl.ds(j * (width // D) + f, count, stride=K), :] = made[:, f * D : (f + 1) * D]
        return carry

    lax.fori_loop(0, 2048 // width, columns, 0)

    def finish(s, carry):
        combined = fm[pl.ds(pl.multiple_of(s * K, K), K), :] + block[start + s, :K].astype(F32)
        block[start + s, :K] = normalized(combined, out_gain[layer])
        return carry

    lax.fori_loop(0, count, finish, 0, unroll=16)


def kernel(
    rows,
    shard,
    slots,
    mixer,
    gains,
    out_gain,
    out,
    block,
    full,
    order,
    inter,
    fm,
    send,
    arrive,
    w_send,
    w_arrive,
    own,
    w_own,
    leave,
):
    dp, fsdp = lax.axis_index("dp"), lax.axis_index("fsdp")
    me = dp * 8 + fsdp
    x, y, z, core = position()
    z_lo = lax.rem(z, 2)
    barrier = pltpu.get_barrier_semaphore()

    def mesh_of(t):
        return {"dp": t // 8, "fsdp": lax.rem(t, 8)}

    def greet(i, carry):
        pl.semaphore_signal(
            barrier, inc=1, device_id=mesh_of(lax.rem(me + i, DEVICES)), device_id_type=MESH
        )
        return carry

    lax.fori_loop(1, DEVICES, greet, 0)

    base = core * HALF
    five, three = pl.ds(base, 5), pl.ds(base + 5, 3)
    quarter = y * 64
    top, bottom = pl.ds(0, 128), pl.ds(128, 128)

    def part(at, size):
        return pl.ds(pl.multiple_of(at, size), size)

    def cols(i):
        return part(i * 256, 256)

    own_copies = []
    for layer in range(LAYERS):
        for j, (slabs, lines) in enumerate(((five, pl.ds(0, N)), (three, part(quarter, 64)))):
            copy = pltpu.make_async_copy(
                shard.at[layer, slabs, lines],
                full.at[layer, slabs, lines, cols(fsdp)],
                w_own.at[layer, j],
            )
            copy.start()
            own_copies.append(copy)
    order[...] = jnp.where(
        lax.broadcasted_iota(jnp.int32, (N, N), 0) == slots[...], 1.0, 0.0
    ).astype(BF16)
    pl.semaphore_wait(barrier, DEVICES - 1)
    sent = []

    def push(layer, slot, source, target, device):
        copy = pltpu.make_async_remote_copy(
            src_ref=source,
            dst_ref=target,
            send_sem=w_send.at[layer, slot],
            recv_sem=w_arrive.at[layer, slot],
            device_id=device,
            device_id_type=MESH,
        )
        copy.start()
        sent.append(copy)
        return copy

    def same(layer, slot, block, device):
        return push(layer, slot, block, block, device)

    right = device_at(x + 1, y, z, core)
    left = device_at(x - 1, y, z, core)
    z_up = device_at(x, y, z + 1, core)
    z_down = device_at(x, y, z - 1, core)
    y_up = device_at(x, y + 1, z, core)
    y_down = device_at(x, y - 1, z, core)
    sibling = device_at(x, y, z, 1 - core)
    x_left, x_right = lax.rem(x + 3, 4), lax.rem(x + 1, 4)
    y_lower, y_upper = lax.rem(y + 3, 4), lax.rem(y + 1, 4)

    def b_x1(layer):
        source, target = shard.at[layer, five], full.at[layer, five, :, cols(fsdp)]
        return [push(layer, 0, source, target, right), push(layer, 1, source, target, left)]

    def a_z(layer):
        return [
            push(
                layer,
                2 + j,
                shard.at[layer, three, part(quarter + 32 * j, 32)],
                full.at[layer, three, part(quarter + 32 * j, 32), cols(fsdp)],
                device,
            )
            for j, device in enumerate((z_up, z_down))
        ]

    def b_x2(layer):
        return [
            same(layer, 4, full.at[layer, five, top, cols(z_lo * 4 + x_left)], right),
            same(layer, 5, full.at[layer, five, bottom, cols(z_lo * 4 + x_right)], left),
        ]

    def a_x1(layer):
        return [
            same(layer, 6 + 2 * j + i, full.at[layer, three, part(quarter, 64), cols(4 * i + x)], device)
            for j, device in enumerate((right, left))
            for i in range(2)
        ]

    def b_z(layer):
        group = part(z_lo * 1024, 1024)
        return [
            same(layer, 10, full.at[layer, five, top, group], z_up),
            same(layer, 11, full.at[layer, five, bottom, group], z_down),
        ]

    def a_x2(layer):
        return [
            same(
                layer,
                12 + 2 * j + i,
                full.at[layer, three, part(quarter + 32 * j, 32), cols(4 * i + origin)],
                device,
            )
            for j, (device, origin) in enumerate(((right, x_left), (left, x_right)))
            for i in range(2)
        ]

    def a_y1(layer):
        lines = full.at[layer, three, part(quarter, 64)]
        return [same(layer, 16, lines, y_up), same(layer, 17, lines, y_down)]

    def b_core(layer):
        return [same(layer, 18, full.at[layer, five], sibling)]

    def a_y2(layer):
        return [
            same(layer, 19, full.at[layer, three, part(y_lower * 64, 32)], y_up),
            same(layer, 20, full.at[layer, three, part(y_upper * 64 + 32, 32)], y_down),
        ]

    def a_core(layer):
        return [same(layer, 21, full.at[layer, three], sibling)]

    def exchange(c):
        def send_one(i, carry):
            t = lax.rem(me + i, DEVICES)
            pltpu.make_async_remote_copy(
                src_ref=rows.at[pl.ds(t * BLOCK + c * STEP, STEP)],
                dst_ref=block.at[pl.ds(c * STEP, STEP), pl.ds(pl.multiple_of(2 * me, 2), 2)],
                send_sem=send.at[c],
                recv_sem=arrive.at[c],
                device_id=mesh_of(t),
                device_id_type=MESH,
            ).start()
            return carry

        lax.fori_loop(1, DEVICES, send_one, 0)
        pltpu.make_async_copy(
            rows.at[pl.ds(me * BLOCK + c * STEP, STEP)],
            block.at[pl.ds(c * STEP, STEP), pl.ds(pl.multiple_of(2 * me, 2), 2)],
            own.at[c],
        ).start()

    def arrived(copies):
        for copy in copies:
            copy.wait_recv()

    def start(layer):
        return b_x1(layer), a_z(layer)

    def spread(layer, b, a):
        arrived(a)
        a = a_x1(layer)
        arrived(b)
        return b_x2(layer), a

    def turn(layer, b, a):
        arrived(a)
        a = a_x2(layer)
        arrived(b)
        b = b_z(layer)
        arrived(a)
        return b, a_y1(layer)

    def close(layer, b, a):
        arrived(b)
        b = b_core(layer)
        arrived(a)
        return b, a_y2(layer)

    zero = start(0)
    for copy in own_copies:
        copy.wait()
    exchange(0)
    zero = spread(0, *zero)
    one = start(1)
    zero = turn(0, *zero)
    exchange(1)
    one = spread(1, *one)
    zero = close(0, *zero)
    one = turn(1, *one)
    exchange(2)
    arrived(zero[1])
    zero = zero[0] + a_core(0)
    one = close(1, *one)
    exchange(3)
    arrived(one[1])
    one = one[0] + a_core(1)
    arrived(zero)
    arrived(one)

    def step(c, carry):
        here = pl.ds(c * STEP, STEP)
        pltpu.make_async_copy(
            rows.at[pl.ds(0, STEP)], block.at[here, pl.ds(0, 2)], own.at[c]
        ).wait()
        others = block.at[here, pl.ds(0, N - 2)]
        pltpu.make_async_copy(others, others, arrive.at[c]).wait()
        for layer in range(LAYERS):
            features_of_block(
                c * STEP,
                STEP,
                block,
                order if layer == 0 else None,
                full,
                layer,
                mixer,
                gains,
                out_gain,
                inter,
                fm,
            )
        pltpu.make_async_copy(block.at[here], out.at[here], leave.at[c]).start()
        return carry

    lax.fori_loop(0, CHUNKS, step, 0)
    for c in range(CHUNKS):
        here = pl.ds(c * STEP, STEP)
        pltpu.make_async_copy(block.at[here], out.at[here], leave.at[c]).wait()
        others = block.at[here, pl.ds(0, N - 2)]
        pltpu.make_async_copy(others, others, send.at[c]).wait()
    for copy in sent:
        copy.wait_send()


def layers(rows, shard, slots, mixer, gains, out_gain):
    vmem = pl.BlockSpec(memory_space=pltpu.VMEM)
    hbm = pl.BlockSpec(memory_space=pl.ANY)
    pushes = 22
    return pl.pallas_call(
        kernel,
        out_shape=jax.ShapeDtypeStruct((BLOCK, N, D), BF16),
        in_specs=[hbm, hbm, vmem, vmem, vmem, vmem],
        out_specs=hbm,
        scratch_shapes=[
            pltpu.VMEM((BLOCK, N, D), BF16),
            pltpu.VMEM((LAYERS, K, N, 2048), BF16),
            pltpu.VMEM((N, N), BF16),
            pltpu.VMEM((2, STEP * K, D), F32),
            pltpu.VMEM((STEP * K, D), F32),
            pltpu.SemaphoreType.DMA((CHUNKS,)),
            pltpu.SemaphoreType.DMA((CHUNKS,)),
            pltpu.SemaphoreType.DMA((LAYERS, pushes)),
            pltpu.SemaphoreType.DMA((LAYERS, pushes)),
            pltpu.SemaphoreType.DMA((CHUNKS,)),
            pltpu.SemaphoreType.DMA((LAYERS, 2)),
            pltpu.SemaphoreType.DMA((CHUNKS,)),
        ],
        compiler_params=pltpu.CompilerParams(
            collective_id=0, has_side_effects=True, vmem_limit_bytes=60 << 20
        ),
    )(rows, shard, slots, mixer, gains, out_gain)


def body(pooled, feature_order, fm_proj, fm_gain, mlp_weight, lcb_weight, out_gain):
    shard = mlp_weight.reshape(LAYERS, N, K, 256).transpose(0, 2, 1, 3)
    gains = fm_gain.reshape(LAYERS, N, K).transpose(0, 2, 1)
    mixer = jnp.concatenate([fm_proj.transpose(0, 2, 1), lcb_weight], axis=1)
    return layers(
        pooled, shard, feature_order.reshape(1, N), mixer, gains, out_gain.reshape(LAYERS, 1, D)
    )


def solution(mesh):
    placed = (P(None, ("dp", "fsdp"), None), P(), P(), P(), P(None, None, "fsdp"), P(), P())
    return jax.shard_map(
        body, mesh=mesh, in_specs=placed, out_specs=P(("dp", "fsdp"), None, None), check_vma=False
    )
```

```python
import jax
import jax.numpy as jnp
from jax import lax
from jax.experimental import pallas as pl
from jax.experimental.pallas import tpu as pltpu
from jax.sharding import PartitionSpec as P

N = 256
D = 128
K = 16
LAYERS = 2
DEVICES = 128
BLOCK = 128
CHUNKS = 4
STEP = BLOCK // CHUNKS
HALF = K // 2
PIECES = 4
PUSHES = 160
MESH = pl.DeviceIdType.MESH
F32 = jnp.float32
BF16 = jnp.bfloat16


def position():
    dp, fsdp = lax.axis_index("dp"), lax.axis_index("fsdp")
    y, z_hi, core = dp // 4, lax.rem(dp // 2, 2), lax.rem(dp, 2)
    z_lo, x = fsdp // 4, lax.rem(fsdp, 4)
    return x, y, z_hi * 2 + z_lo, core


def device_at(x, y, z, core):
    x, y, z = lax.rem(x + 4, 4), lax.rem(y + 4, 4), lax.rem(z + 4, 4)
    return {"dp": (y * 2 + z // 2) * 2 + core, "fsdp": lax.rem(z, 2) * 4 + x}


def normalized(values, gain):
    center = jnp.mean(values, axis=-1, keepdims=True)
    apart = values - center
    spread = jnp.mean(apart * apart, axis=-1, keepdims=True)
    return (apart * lax.rsqrt(spread + 1e-05) * gain).astype(BF16)


def features_of_block(start, count, block, order, weights, layer, mixer, gains, out_gain, inter, fm):
    def pair(i, carry):
        a = start + 2 * i
        both = jnp.concatenate([block[a], block[a + 1]], axis=1)
        if order is not None:
            both = jnp.dot(order[...], both, preferred_element_type=F32).astype(BF16)
        mixed = jnp.dot(mixer[layer], both, preferred_element_type=F32)
        projected = mixed[:K].astype(BF16)
        none = jnp.zeros((K, D), BF16)
        apart = jnp.concatenate(
            [
                jnp.concatenate([projected[:, :D], none], axis=1),
                jnp.concatenate([none, projected[:, D:]], axis=1),
            ],
            axis=0,
        )
        products = lax.dot_general(
            apart, both, (((1,), (1,)), ((), ())), preferred_element_type=F32
        )
        for half in range(2):
            inter[half, pl.ds(pl.multiple_of(2 * i * K, 2 * K), 2 * K), :] = products[
                :, half * D : (half + 1) * D
            ]
        for s, at in ((a, 0), (a + 1, D)):
            rows = both[:, at : at + D]
            combined = mixed[K:, at : at + D] + rows[K:].astype(F32)
            block[s, :K] = rows[:K]
            block[s, K:] = normalized(combined, out_gain[layer])
        return carry

    lax.fori_loop(0, count // 2, pair, 0, unroll=8)

    def taken(k):
        return jnp.concatenate(
            [inter[half, pl.ds(k, count, stride=K), :] for half in range(2)], axis=1
        )

    total = jnp.zeros((count, N), F32)
    for k in range(K):
        total += taken(k)
    center = jnp.sum(total, axis=-1, keepdims=True) * (1.0 / (N * K))
    squares = jnp.zeros((count, N), F32)
    for k in range(K):
        apart = taken(k) - center
        squares += apart * apart
    scale = lax.rsqrt(jnp.sum(squares, axis=-1, keepdims=True) * (1.0 / (N * K)) + 1e-05)
    width = 1024

    def columns(j, carry):
        at = pl.multiple_of(j * width, width)
        made = jnp.zeros((count, width), F32)
        for k in range(K):
            apart = taken(k) - center
            normed = (apart * scale * gains[layer, k : k + 1, :]).astype(BF16)
            made += jnp.dot(
                normed, weights[layer, k, :, pl.ds(at, width)], preferred_element_type=F32
            )
        made = made.astype(BF16).astype(F32)
        for f in range(width // D):
            fm[pl.ds(j * (width // D) + f, count, stride=K), :] = made[:, f * D : (f + 1) * D]
        return carry

    lax.fori_loop(0, 2048 // width, columns, 0)

    def finish(s, carry):
        combined = fm[pl.ds(pl.multiple_of(s * K, K), K), :] + block[start + s, :K].astype(F32)
        block[start + s, :K] = normalized(combined, out_gain[layer])
        return carry

    lax.fori_loop(0, count, finish, 0, unroll=16)


def kernel(
    rows,
    shard,
    slots,
    mixer,
    gains,
    out_gain,
    out,
    block,
    full,
    order,
    inter,
    fm,
    send,
    arrive,
    w_send,
    w_arrive,
    own,
    w_own,
    leave,
):
    dp, fsdp = lax.axis_index("dp"), lax.axis_index("fsdp")
    me = dp * 8 + fsdp
    x, y, z, core = position()
    z_lo = lax.rem(z, 2)
    barrier = pltpu.get_barrier_semaphore()

    def mesh_of(t):
        return {"dp": t // 8, "fsdp": lax.rem(t, 8)}

    def greet(i, carry):
        pl.semaphore_signal(
            barrier, inc=1, device_id=mesh_of(lax.rem(me + i, DEVICES)), device_id_type=MESH
        )
        return carry

    lax.fori_loop(1, DEVICES, greet, 0)

    base = core * HALF
    five, three = pl.ds(base, 5), pl.ds(base + 5, 3)
    quarter = y * 64
    top, bottom = pl.ds(0, 128), pl.ds(128, 128)

    def part(at, size):
        return pl.ds(pl.multiple_of(at, size), size)

    def cols(i):
        return part(i * 256, 256)

    own_copies = []
    for layer in range(LAYERS):
        for j, (slabs, lines) in enumerate(((five, pl.ds(0, N)), (three, part(quarter, 64)))):
            copy = pltpu.make_async_copy(
                shard.at[layer, slabs, lines],
                full.at[layer, slabs, lines, cols(fsdp)],
                w_own.at[layer, j],
            )
            copy.start()
            own_copies.append(copy)
    order[...] = jnp.where(
        lax.broadcasted_iota(jnp.int32, (N, N), 0) == slots[...], 1.0, 0.0
    ).astype(BF16)
    pl.semaphore_wait(barrier, DEVICES - 1)
    sent = []

    def push(source, target, device):
        copy = pltpu.make_async_remote_copy(
            src_ref=source,
            dst_ref=target,
            send_sem=w_send.at[len(sent)],
            recv_sem=w_arrive.at[len(sent)],
            device_id=device,
            device_id_type=MESH,
        )
        copy.start()
        sent.append(copy)
        return copy

    def same(block, device):
        return push(block, block, device)

    right = device_at(x + 1, y, z, core)
    left = device_at(x - 1, y, z, core)
    z_up = device_at(x, y, z + 1, core)
    z_down = device_at(x, y, z - 1, core)
    y_up = device_at(x, y + 1, z, core)
    y_down = device_at(x, y - 1, z, core)
    sibling = device_at(x, y, z, 1 - core)
    x_left, x_right = lax.rem(x + 3, 4), lax.rem(x + 1, 4)
    y_lower, y_upper = lax.rem(y + 3, 4), lax.rem(y + 1, 4)

    quarter_halves = [part(quarter + 32 * j, 32) for j in range(2)]
    group = part(z_lo * 1024, 1024)

    def along_x_z(layer, slab):
        source, target = shard.at[layer, slab], full.at[layer, slab, :, cols(fsdp)]
        yield [push(source, target, right), push(source, target, left)]
        yield [
            same(full.at[layer, slab, top, cols(z_lo * 4 + x_left)], right),
            same(full.at[layer, slab, bottom, cols(z_lo * 4 + x_right)], left),
        ]
        yield [
            same(full.at[layer, slab, top, group], z_up),
            same(full.at[layer, slab, bottom, group], z_down),
        ]
        yield [same(full.at[layer, slab], sibling)]

    def along_z_x_y(layer, slab):
        yield [
            push(
                shard.at[layer, slab, quarter_halves[j]],
                full.at[layer, slab, quarter_halves[j], cols(fsdp)],
                device,
            )
            for j, device in enumerate((z_up, z_down))
        ]
        yield [
            same(full.at[layer, slab, part(quarter, 64), cols(4 * i + x)], device)
            for device in (right, left)
            for i in range(2)
        ]
        yield [
            same(full.at[layer, slab, quarter_halves[j], cols(4 * i + origin)], device)
            for j, (device, origin) in enumerate(((right, x_left), (left, x_right)))
            for i in range(2)
        ]
        lines = full.at[layer, slab, part(quarter, 64)]
        yield [same(lines, y_up), same(lines, y_down)]
        yield [
            same(full.at[layer, slab, part(y_lower * 64, 32)], y_up),
            same(full.at[layer, slab, part(y_upper * 64 + 32, 32)], y_down),
        ]
        yield [same(full.at[layer, slab], sibling)]

    def exchange(piece):
        c, first = piece // PIECES, piece % PIECES * (DEVICES // PIECES)

        def send_one(i, carry):
            t = lax.rem(me + i * 37, DEVICES)
            pltpu.make_async_remote_copy(
                src_ref=rows.at[pl.ds(t * BLOCK + c * STEP, STEP)],
                dst_ref=block.at[pl.ds(c * STEP, STEP), pl.ds(pl.multiple_of(2 * me, 2), 2)],
                send_sem=send.at[c],
                recv_sem=arrive.at[c],
                device_id=mesh_of(t),
                device_id_type=MESH,
            ).start()
            return carry

        lax.fori_loop(max(first, 1), first + DEVICES // PIECES, send_one, 0)
        if first == 0:
            pltpu.make_async_copy(
                rows.at[pl.ds(me * BLOCK + c * STEP, STEP)],
                block.at[pl.ds(c * STEP, STEP), pl.ds(pl.multiple_of(2 * me, 2), 2)],
                own.at[c],
            ).start()

    ways = []
    for layer in range(LAYERS):
        for i in range(5):
            ways.append([layer * 5 + i, along_x_z(layer, base + i), []])
        for i in range(3):
            ways.append([layer * 3 + i, along_z_x_y(layer, base + 5 + i), []])
    ways.sort(key=lambda way: way[0])
    pieces = CHUNKS * PIECES
    ticks, issued = 0, 0
    while ways:
        for way in ways:
            if way[0] <= ticks and (ticks - way[0]) % 2 == 0:
                for copy in way[2]:
                    copy.wait_recv()
                way[2] = next(way[1], None)
        ways = [way for way in ways if way[2] is not None]
        if ticks == 0:
            for copy in own_copies:
                copy.wait()
        wanted = min(pieces, (ticks + 1) // 2)
        while issued < wanted:
            exchange(issued)
            issued += 1
        ticks += 1
    while issued < pieces:
        exchange(issued)
        issued += 1

    def step(c, carry):
        here = pl.ds(c * STEP, STEP)
        pltpu.make_async_copy(
            rows.at[pl.ds(0, STEP)], block.at[here, pl.ds(0, 2)], own.at[c]
        ).wait()
        others = block.at[here, pl.ds(0, N - 2)]
        pltpu.make_async_copy(others, others, arrive.at[c]).wait()
        for layer in range(LAYERS):
            features_of_block(
                c * STEP,
                STEP,
                block,
                order if layer == 0 else None,
                full,
                layer,
                mixer,
                gains,
                out_gain,
                inter,
                fm,
            )
        pltpu.make_async_copy(block.at[here], out.at[here], leave.at[c]).start()
        return carry

    lax.fori_loop(0, CHUNKS, step, 0)
    for c in range(CHUNKS):
        here = pl.ds(c * STEP, STEP)
        pltpu.make_async_copy(block.at[here], out.at[here], leave.at[c]).wait()
        others = block.at[here, pl.ds(0, N - 2)]
        pltpu.make_async_copy(others, others, send.at[c]).wait()
    for copy in sent:
        copy.wait_send()


def layers(rows, shard, slots, mixer, gains, out_gain):
    vmem = pl.BlockSpec(memory_space=pltpu.VMEM)
    hbm = pl.BlockSpec(memory_space=pl.ANY)
    return pl.pallas_call(
        kernel,
        out_shape=jax.ShapeDtypeStruct((BLOCK, N, D), BF16),
        in_specs=[hbm, hbm, vmem, vmem, vmem, vmem],
        out_specs=hbm,
        scratch_shapes=[
            pltpu.VMEM((BLOCK, N, D), BF16),
            pltpu.VMEM((LAYERS, K, N, 2048), BF16),
            pltpu.VMEM((N, N), BF16),
            pltpu.VMEM((2, STEP * K, D), F32),
            pltpu.VMEM((STEP * K, D), F32),
            pltpu.SemaphoreType.DMA((CHUNKS,)),
            pltpu.SemaphoreType.DMA((CHUNKS,)),
            pltpu.SemaphoreType.DMA((PUSHES,)),
            pltpu.SemaphoreType.DMA((PUSHES,)),
            pltpu.SemaphoreType.DMA((CHUNKS,)),
            pltpu.SemaphoreType.DMA((LAYERS, 2)),
            pltpu.SemaphoreType.DMA((CHUNKS,)),
        ],
        compiler_params=pltpu.CompilerParams(
            collective_id=0, has_side_effects=True, vmem_limit_bytes=60 << 20
        ),
    )(rows, shard, slots, mixer, gains, out_gain)


def body(pooled, feature_order, fm_proj, fm_gain, mlp_weight, lcb_weight, out_gain):
    shard = mlp_weight.reshape(LAYERS, N, K, 256).transpose(0, 2, 1, 3)
    gains = fm_gain.reshape(LAYERS, N, K).transpose(0, 2, 1)
    mixer = jnp.concatenate([fm_proj.transpose(0, 2, 1), lcb_weight], axis=1)
    return layers(
        pooled, shard, feature_order.reshape(1, N), mixer, gains, out_gain.reshape(LAYERS, 1, D)
    )


def solution(mesh):
    placed = (P(None, ("dp", "fsdp"), None), P(), P(), P(), P(None, None, "fsdp"), P(), P())
    return jax.shard_map(
        body, mesh=mesh, in_specs=placed, out_specs=P(("dp", "fsdp"), None, None), check_vma=False
    )
```

```python
import jax
import jax.numpy as jnp
from jax import lax
from jax.experimental import pallas as pl
from jax.experimental.pallas import tpu as pltpu
from jax.sharding import PartitionSpec as P

N = 256
D = 128
K = 16
LAYERS = 2
DEVICES = 128
BLOCK = 128
CHUNKS = 4
STEP = BLOCK // CHUNKS
HALF = K // 2
PIECES = 4
PUSHES = 160
MESH = pl.DeviceIdType.MESH
F32 = jnp.float32
BF16 = jnp.bfloat16


def position():
    dp, fsdp = lax.axis_index("dp"), lax.axis_index("fsdp")
    y, z_hi, core = dp // 4, lax.rem(dp // 2, 2), lax.rem(dp, 2)
    z_lo, x = fsdp // 4, lax.rem(fsdp, 4)
    return x, y, z_hi * 2 + z_lo, core


def device_at(x, y, z, core):
    x, y, z = lax.rem(x + 4, 4), lax.rem(y + 4, 4), lax.rem(z + 4, 4)
    return {"dp": (y * 2 + z // 2) * 2 + core, "fsdp": lax.rem(z, 2) * 4 + x}


def normalized(values, gain):
    center = jnp.mean(values, axis=-1, keepdims=True)
    apart = values - center
    spread = jnp.mean(apart * apart, axis=-1, keepdims=True)
    return (apart * lax.rsqrt(spread + 1e-05) * gain).astype(BF16)


def features_of_block(start, count, block, order, weights, layer, mixer, gains, out_gain, inter, fm):
    def pair(i, carry):
        a = start + 2 * i
        both = jnp.concatenate([block[a], block[a + 1]], axis=1)
        if order is not None:
            both = jnp.dot(order[...], both, preferred_element_type=F32).astype(BF16)
        mixed = jnp.dot(mixer[layer], both, preferred_element_type=F32)
        projected = mixed[:K].astype(BF16)
        none = jnp.zeros((K, D), BF16)
        apart = jnp.concatenate(
            [
                jnp.concatenate([projected[:, :D], none], axis=1),
                jnp.concatenate([none, projected[:, D:]], axis=1),
            ],
            axis=0,
        )
        products = lax.dot_general(
            apart, both, (((1,), (1,)), ((), ())), preferred_element_type=F32
        )
        for half in range(2):
            inter[half, pl.ds(pl.multiple_of(2 * i * K, 2 * K), 2 * K), :] = products[
                :, half * D : (half + 1) * D
            ]
        for s, at in ((a, 0), (a + 1, D)):
            rows = both[:, at : at + D]
            combined = mixed[K:, at : at + D] + rows[K:].astype(F32)
            block[s, :K] = rows[:K]
            block[s, K:] = normalized(combined, out_gain[layer])
        return carry

    lax.fori_loop(0, count // 2, pair, 0, unroll=8)

    def taken(k):
        return jnp.concatenate(
            [inter[half, pl.ds(k, count, stride=K), :] for half in range(2)], axis=1
        )

    total = jnp.zeros((count, N), F32)
    for k in range(K):
        total += taken(k)
    center = jnp.sum(total, axis=-1, keepdims=True) * (1.0 / (N * K))
    squares = jnp.zeros((count, N), F32)
    for k in range(K):
        apart = taken(k) - center
        squares += apart * apart
    scale = lax.rsqrt(jnp.sum(squares, axis=-1, keepdims=True) * (1.0 / (N * K)) + 1e-05)
    width = 1024

    def columns(j, carry):
        at = pl.multiple_of(j * width, width)
        made = jnp.zeros((count, width), F32)
        for k in range(K):
            apart = taken(k) - center
            normed = (apart * scale * gains[layer, k : k + 1, :]).astype(BF16)
            made += jnp.dot(
                normed, weights[layer, k, :, pl.ds(at, width)], preferred_element_type=F32
            )
        made = made.astype(BF16).astype(F32)
        for f in range(width // D):
            fm[pl.ds(j * (width // D) + f, count, stride=K), :] = made[:, f * D : (f + 1) * D]
        return carry

    lax.fori_loop(0, 2048 // width, columns, 0)

    def finish(s, carry):
        combined = fm[pl.ds(pl.multiple_of(s * K, K), K), :] + block[start + s, :K].astype(F32)
        block[start + s, :K] = normalized(combined, out_gain[layer])
        return carry

    lax.fori_loop(0, count, finish, 0, unroll=16)


def kernel(
    rows,
    shard,
    slots,
    fm_proj,
    lcb_weight,
    fm_gain,
    out_gain,
    block,
    full,
    order,
    mixer,
    gains,
    inter,
    fm,
    send,
    arrive,
    w_send,
    w_arrive,
    own,
    w_own,
):
    dp, fsdp = lax.axis_index("dp"), lax.axis_index("fsdp")
    me = dp * 8 + fsdp
    x, y, z, core = position()
    z_lo = lax.rem(z, 2)
    barrier = pltpu.get_barrier_semaphore()

    def mesh_of(t):
        return {"dp": t // 8, "fsdp": lax.rem(t, 8)}

    def greet(i, carry):
        pl.semaphore_signal(
            barrier, inc=1, device_id=mesh_of(lax.rem(me + i, DEVICES)), device_id_type=MESH
        )
        return carry

    lax.fori_loop(1, DEVICES, greet, 0)

    base = core * HALF
    five, three = pl.ds(base, 5), pl.ds(base + 5, 3)
    quarter = y * 64
    top, bottom = pl.ds(0, 128), pl.ds(128, 128)

    def part(at, size):
        return pl.ds(pl.multiple_of(at, size), size)

    def cols(i):
        return part(i * 256, 256)

    own_copies = []
    for layer in range(LAYERS):
        for j, (slabs, lines) in enumerate(((five, pl.ds(0, N)), (three, part(quarter, 64)))):
            copy = pltpu.make_async_copy(
                shard.at[layer, slabs, lines],
                full.at[layer, slabs, lines, cols(fsdp)],
                w_own.at[layer, j],
            )
            copy.start()
            own_copies.append(copy)
    order[...] = jnp.where(
        lax.broadcasted_iota(jnp.int32, (N, N), 0) == slots[...], 1.0, 0.0
    ).astype(BF16)
    pl.semaphore_wait(barrier, DEVICES - 1)
    sent = []

    def push(source, target, device):
        copy = pltpu.make_async_remote_copy(
            src_ref=source,
            dst_ref=target,
            send_sem=w_send.at[len(sent)],
            recv_sem=w_arrive.at[len(sent)],
            device_id=device,
            device_id_type=MESH,
        )
        copy.start()
        sent.append(copy)
        return copy

    def same(block, device):
        return push(block, block, device)

    right = device_at(x + 1, y, z, core)
    left = device_at(x - 1, y, z, core)
    z_up = device_at(x, y, z + 1, core)
    z_down = device_at(x, y, z - 1, core)
    y_up = device_at(x, y + 1, z, core)
    y_down = device_at(x, y - 1, z, core)
    sibling = device_at(x, y, z, 1 - core)
    x_left, x_right = lax.rem(x + 3, 4), lax.rem(x + 1, 4)
    y_lower, y_upper = lax.rem(y + 3, 4), lax.rem(y + 1, 4)

    quarter_halves = [part(quarter + 32 * j, 32) for j in range(2)]
    group = part(z_lo * 1024, 1024)

    def along_x_z(layer, slab):
        source, target = shard.at[layer, slab], full.at[layer, slab, :, cols(fsdp)]
        yield [push(source, target, right), push(source, target, left)]
        yield [
            same(full.at[layer, slab, top, cols(z_lo * 4 + x_left)], right),
            same(full.at[layer, slab, bottom, cols(z_lo * 4 + x_right)], left),
        ]
        yield [
            same(full.at[layer, slab, top, group], z_up),
            same(full.at[layer, slab, bottom, group], z_down),
        ]
        yield [same(full.at[layer, slab], sibling)]

    def along_z_x_y(layer, slab):
        yield [
            push(
                shard.at[layer, slab, quarter_halves[j]],
                full.at[layer, slab, quarter_halves[j], cols(fsdp)],
                device,
            )
            for j, device in enumerate((z_up, z_down))
        ]
        yield [
            same(full.at[layer, slab, part(quarter, 64), cols(4 * i + x)], device)
            for device in (right, left)
            for i in range(2)
        ]
        yield [
            same(full.at[layer, slab, quarter_halves[j], cols(4 * i + origin)], device)
            for j, (device, origin) in enumerate(((right, x_left), (left, x_right)))
            for i in range(2)
        ]
        lines = full.at[layer, slab, part(quarter, 64)]
        yield [same(lines, y_up), same(lines, y_down)]
        yield [
            same(full.at[layer, slab, part(y_lower * 64, 32)], y_up),
            same(full.at[layer, slab, part(y_upper * 64 + 32, 32)], y_down),
        ]
        yield [same(full.at[layer, slab], sibling)]

    def exchange(piece):
        c, first = piece // PIECES, piece % PIECES * (DEVICES // PIECES)

        def send_one(i, carry):
            t = lax.rem(me + i * 37, DEVICES)
            pltpu.make_async_remote_copy(
                src_ref=rows.at[pl.ds(t * BLOCK + c * STEP, STEP)],
                dst_ref=block.at[pl.ds(c * STEP, STEP), pl.ds(pl.multiple_of(2 * me, 2), 2)],
                send_sem=send.at[c],
                recv_sem=arrive.at[c],
                device_id=mesh_of(t),
                device_id_type=MESH,
            ).start()
            return carry

        lax.fori_loop(max(first, 1), first + DEVICES // PIECES, send_one, 0)
        if first == 0:
            pltpu.make_async_copy(
                rows.at[pl.ds(me * BLOCK + c * STEP, STEP)],
                block.at[pl.ds(c * STEP, STEP), pl.ds(pl.multiple_of(2 * me, 2), 2)],
                own.at[c],
            ).start()

    ways = []
    for layer in range(LAYERS):
        for i in range(5):
            ways.append([layer * 5 + i, along_x_z(layer, base + i), []])
        for i in range(3):
            ways.append([layer * 3 + i, along_z_x_y(layer, base + 5 + i), []])
    ways.sort(key=lambda way: way[0])
    pieces = CHUNKS * PIECES
    ticks, issued = 0, 0
    while ways:
        for way in ways:
            if way[0] <= ticks and (ticks - way[0]) % 2 == 0:
                for copy in way[2]:
                    copy.wait_recv()
                way[2] = next(way[1], None)
        ways = [way for way in ways if way[2] is not None]
        if ticks == 0:
            for copy in own_copies:
                copy.wait()
            for layer in range(LAYERS):
                mixer[layer, :K] = fm_proj[layer]
                mixer[layer, K:] = lcb_weight[layer]
                gains[layer] = fm_gain[layer].T
        wanted = min(pieces, (ticks + 1) // 2)
        while issued < wanted:
            exchange(issued)
            issued += 1
        ticks += 1
    while issued < pieces:
        exchange(issued)
        issued += 1

    def step(c, carry):
        here = pl.ds(c * STEP, STEP)
        pltpu.make_async_copy(
            rows.at[pl.ds(0, STEP)], block.at[here, pl.ds(0, 2)], own.at[c]
        ).wait()
        others = block.at[here, pl.ds(0, N - 2)]
        pltpu.make_async_copy(others, others, arrive.at[c]).wait()
        for layer in range(LAYERS):
            features_of_block(
                c * STEP,
                STEP,
                block,
                order if layer == 0 else None,
                full,
                layer,
                mixer,
                gains,
                out_gain,
                inter,
                fm,
            )
        return carry

    lax.fori_loop(0, CHUNKS, step, 0)
    for c in range(CHUNKS):
        here = pl.ds(c * STEP, STEP)
        others = block.at[here, pl.ds(0, N - 2)]
        pltpu.make_async_copy(others, others, send.at[c]).wait()
    for copy in sent:
        copy.wait_send()


def layers(rows, shard, slots, fm_proj, lcb_weight, fm_gain, out_gain):
    vmem = pl.BlockSpec(memory_space=pltpu.VMEM)
    hbm = pl.BlockSpec(memory_space=pl.ANY)
    return pl.pallas_call(
        kernel,
        out_shape=pltpu.VMEM((BLOCK, N, D), BF16),
        in_specs=[hbm, hbm, vmem, vmem, vmem, vmem, vmem],
        out_specs=vmem,
        scratch_shapes=[
            pltpu.VMEM((LAYERS, K, N, 2048), BF16),
            pltpu.VMEM((N, N), BF16),
            pltpu.VMEM((LAYERS, N, N), BF16),
            pltpu.VMEM((LAYERS, K, N), F32),
            pltpu.VMEM((2, STEP * K, D), F32),
            pltpu.VMEM((STEP * K, D), F32),
            pltpu.SemaphoreType.DMA((CHUNKS,)),
            pltpu.SemaphoreType.DMA((CHUNKS,)),
            pltpu.SemaphoreType.DMA((PUSHES,)),
            pltpu.SemaphoreType.DMA((PUSHES,)),
            pltpu.SemaphoreType.DMA((CHUNKS,)),
            pltpu.SemaphoreType.DMA((LAYERS, 2)),
        ],
        compiler_params=pltpu.CompilerParams(
            collective_id=0, has_side_effects=True, vmem_limit_bytes=40 << 20
        ),
    )(rows, shard, slots, fm_proj, lcb_weight, fm_gain, out_gain)


def body(pooled, feature_order, fm_proj, fm_gain, mlp_weight, lcb_weight, out_gain):
    shard = mlp_weight.reshape(LAYERS, N, K, 256).transpose(0, 2, 1, 3)
    gains = fm_gain.reshape(LAYERS, N, K)
    slots = feature_order.reshape(1, N)
    out_gains = out_gain.reshape(LAYERS, 1, D)
    projections = fm_proj.transpose(0, 2, 1)
    return layers(pooled, shard, slots, projections, lcb_weight, gains, out_gains)


def solution(mesh):
    placed = (P(None, ("dp", "fsdp"), None), P(), P(), P(), P(None, None, "fsdp"), P(), P())
    return jax.shard_map(
        body, mesh=mesh, in_specs=placed, out_specs=P(("dp", "fsdp"), None, None), check_vma=False
    )
```

```python
import jax
import jax.numpy as jnp
from jax import lax
from jax.experimental import pallas as pl
from jax.experimental.pallas import tpu as pltpu
from jax.sharding import PartitionSpec as P

N = 256
D = 128
K = 16
LAYERS = 2
DEVICES = 128
BLOCK = 128
CHUNKS = 4
STEP = BLOCK // CHUNKS
HALF = K // 2
PIECES = 4
PUSHES = 160
MESH = pl.DeviceIdType.MESH
F32 = jnp.float32
BF16 = jnp.bfloat16


def position():
    dp, fsdp = lax.axis_index("dp"), lax.axis_index("fsdp")
    y, z_hi, core = dp // 4, lax.rem(dp // 2, 2), lax.rem(dp, 2)
    z_lo, x = fsdp // 4, lax.rem(fsdp, 4)
    return x, y, z_hi * 2 + z_lo, core


def device_at(x, y, z, core):
    x, y, z = lax.rem(x + 4, 4), lax.rem(y + 4, 4), lax.rem(z + 4, 4)
    return {"dp": (y * 2 + z // 2) * 2 + core, "fsdp": lax.rem(z, 2) * 4 + x}


def normalized(values, gain):
    center = jnp.mean(values, axis=-1, keepdims=True)
    apart = values - center
    spread = jnp.mean(apart * apart, axis=-1, keepdims=True)
    return (apart * lax.rsqrt(spread + 1e-05) * gain).astype(BF16)


def features_of_block(start, count, block, order, weights, layer, mixer, gains, out_gain, inter, fm):
    def pair(i, carry):
        a = start + 2 * i
        both = jnp.concatenate([block[a], block[a + 1]], axis=1)
        if order is not None:
            both = jnp.dot(order[...], both, preferred_element_type=F32).astype(BF16)
        mixed = jnp.dot(mixer[layer], both, preferred_element_type=F32)
        projected = mixed[:K].astype(BF16)
        none = jnp.zeros((K, D), BF16)
        apart = jnp.concatenate(
            [
                jnp.concatenate([projected[:, :D], none], axis=1),
                jnp.concatenate([none, projected[:, D:]], axis=1),
            ],
            axis=0,
        )
        products = lax.dot_general(
            apart, both, (((1,), (1,)), ((), ())), preferred_element_type=F32
        )
        for half in range(2):
            inter[half, pl.ds(pl.multiple_of(2 * i * K, 2 * K), 2 * K), :] = products[
                :, half * D : (half + 1) * D
            ]
        for s, at in ((a, 0), (a + 1, D)):
            rows = both[:, at : at + D]
            combined = mixed[K:, at : at + D] + rows[K:].astype(F32)
            block[s, :K] = rows[:K]
            block[s, K:] = normalized(combined, out_gain[layer])
        return carry

    lax.fori_loop(0, count // 2, pair, 0, unroll=8)

    def taken(k):
        return jnp.concatenate(
            [inter[half, pl.ds(k, count, stride=K), :] for half in range(2)], axis=1
        )

    total = jnp.zeros((count, N), F32)
    for k in range(K):
        total += taken(k)
    center = jnp.sum(total, axis=-1, keepdims=True) * (1.0 / (N * K))
    squares = jnp.zeros((count, N), F32)
    for k in range(K):
        apart = taken(k) - center
        squares += apart * apart
    scale = lax.rsqrt(jnp.sum(squares, axis=-1, keepdims=True) * (1.0 / (N * K)) + 1e-05)
    width = 1024

    def columns(j, carry):
        at = pl.multiple_of(j * width, width)
        made = jnp.zeros((count, width), F32)
        for k in range(K):
            apart = taken(k) - center
            normed = (apart * scale * gains[layer, k : k + 1, :]).astype(BF16)
            made += jnp.dot(
                normed, weights[layer, k, :, pl.ds(at, width)], preferred_element_type=F32
            )
        made = made.astype(BF16).astype(F32)
        for f in range(width // D):
            fm[pl.ds(j * (width // D) + f, count, stride=K), :] = made[:, f * D : (f + 1) * D]
        return carry

    lax.fori_loop(0, 2048 // width, columns, 0)

    def finish(s, carry):
        combined = fm[pl.ds(pl.multiple_of(s * K, K), K), :] + block[start + s, :K].astype(F32)
        block[start + s, :K] = normalized(combined, out_gain[layer])
        return carry

    lax.fori_loop(0, count, finish, 0, unroll=16)


def kernel(
    rows,
    shard,
    slots,
    fm_proj,
    lcb_weight,
    fm_gain,
    out_gain,
    block,
    full,
    order,
    mixer,
    gains,
    inter,
    fm,
    send,
    arrive,
    w_send,
    w_arrive,
    own,
    w_own,
):
    dp, fsdp = lax.axis_index("dp"), lax.axis_index("fsdp")
    me = dp * 8 + fsdp
    x, y, z, core = position()
    z_lo = lax.rem(z, 2)
    barrier = pltpu.get_barrier_semaphore()

    def mesh_of(t):
        return {"dp": t // 8, "fsdp": lax.rem(t, 8)}

    def greet(i, carry):
        pl.semaphore_signal(
            barrier, inc=1, device_id=mesh_of(lax.rem(me + i, DEVICES)), device_id_type=MESH
        )
        return carry

    lax.fori_loop(1, DEVICES, greet, 0)

    base = core * HALF
    five, three = pl.ds(base, 5), pl.ds(base + 5, 3)
    quarter = y * 64
    top, bottom = pl.ds(0, 128), pl.ds(128, 128)

    def part(at, size):
        return pl.ds(pl.multiple_of(at, size), size)

    def cols(i):
        return part(i * 256, 256)

    own_copies = []
    for layer in range(LAYERS):
        for j, (taken, slabs, lines) in enumerate(
            (
                (pl.ds(0, 5), five, pl.ds(0, N)),
                (pl.ds(5, 3), three, part(quarter, 64)),
            )
        ):
            copy = pltpu.make_async_copy(
                shard.at[layer, taken, lines],
                full.at[layer, slabs, lines, cols(fsdp)],
                w_own.at[layer, j],
            )
            copy.start()
            own_copies.append(copy)
    order[...] = jnp.where(
        lax.broadcasted_iota(jnp.int32, (N, N), 0) == slots[...], 1.0, 0.0
    ).astype(BF16)
    pl.semaphore_wait(barrier, DEVICES - 1)
    sent = []

    def push(source, target, device):
        copy = pltpu.make_async_remote_copy(
            src_ref=source,
            dst_ref=target,
            send_sem=w_send.at[len(sent)],
            recv_sem=w_arrive.at[len(sent)],
            device_id=device,
            device_id_type=MESH,
        )
        copy.start()
        sent.append(copy)
        return copy

    def same(block, device):
        return push(block, block, device)

    right = device_at(x + 1, y, z, core)
    left = device_at(x - 1, y, z, core)
    z_up = device_at(x, y, z + 1, core)
    z_down = device_at(x, y, z - 1, core)
    y_up = device_at(x, y + 1, z, core)
    y_down = device_at(x, y - 1, z, core)
    sibling = device_at(x, y, z, 1 - core)
    x_left, x_right = lax.rem(x + 3, 4), lax.rem(x + 1, 4)
    y_lower, y_upper = lax.rem(y + 3, 4), lax.rem(y + 1, 4)

    quarter_halves = [part(quarter + 32 * j, 32) for j in range(2)]
    group = part(z_lo * 1024, 1024)

    def along_x_z(layer, slab):
        source, target = shard.at[layer, slab - base], full.at[layer, slab, :, cols(fsdp)]
        yield [push(source, target, right), push(source, target, left)]
        yield [
            same(full.at[layer, slab, top, cols(z_lo * 4 + x_left)], right),
            same(full.at[layer, slab, bottom, cols(z_lo * 4 + x_right)], left),
        ]
        yield [
            same(full.at[layer, slab, top, group], z_up),
            same(full.at[layer, slab, bottom, group], z_down),
        ]
        yield [same(full.at[layer, slab], sibling)]

    def along_z_x_y(layer, slab):
        yield [
            push(
                shard.at[layer, slab - base, quarter_halves[j]],
                full.at[layer, slab, quarter_halves[j], cols(fsdp)],
                device,
            )
            for j, device in enumerate((z_up, z_down))
        ]
        yield [
            same(full.at[layer, slab, part(quarter, 64), cols(4 * i + x)], device)
            for device in (right, left)
            for i in range(2)
        ]
        yield [
            same(full.at[layer, slab, quarter_halves[j], cols(4 * i + origin)], device)
            for j, (device, origin) in enumerate(((right, x_left), (left, x_right)))
            for i in range(2)
        ]
        lines = full.at[layer, slab, part(quarter, 64)]
        yield [same(lines, y_up), same(lines, y_down)]
        yield [
            same(full.at[layer, slab, part(y_lower * 64, 32)], y_up),
            same(full.at[layer, slab, part(y_upper * 64 + 32, 32)], y_down),
        ]
        yield [same(full.at[layer, slab], sibling)]

    def exchange(piece):
        c, first = piece // PIECES, piece % PIECES * (DEVICES // PIECES)

        def send_one(i, carry):
            t = lax.rem(me + i * 37, DEVICES)
            pltpu.make_async_remote_copy(
                src_ref=rows.at[pl.ds(t * BLOCK + c * STEP, STEP)],
                dst_ref=block.at[pl.ds(c * STEP, STEP), pl.ds(pl.multiple_of(2 * me, 2), 2)],
                send_sem=send.at[c],
                recv_sem=arrive.at[c],
                device_id=mesh_of(t),
                device_id_type=MESH,
            ).start()
            return carry

        lax.fori_loop(max(first, 1), first + DEVICES // PIECES, send_one, 0)
        if first == 0:
            pltpu.make_async_copy(
                rows.at[pl.ds(me * BLOCK + c * STEP, STEP)],
                block.at[pl.ds(c * STEP, STEP), pl.ds(pl.multiple_of(2 * me, 2), 2)],
                own.at[c],
            ).start()

    ways = []
    for layer in range(LAYERS):
        for i in range(5):
            ways.append([layer * 5 + i, along_x_z(layer, base + i), []])
        for i in range(3):
            ways.append([layer * 3 + i, along_z_x_y(layer, base + 5 + i), []])
    ways.sort(key=lambda way: way[0])
    pieces = CHUNKS * PIECES
    ticks, issued = 0, 0
    while ways:
        for way in ways:
            if way[0] <= ticks and (ticks - way[0]) % 2 == 0:
                for copy in way[2]:
                    copy.wait_recv()
                way[2] = next(way[1], None)
        ways = [way for way in ways if way[2] is not None]
        if ticks == 0:
            for copy in own_copies:
                copy.wait()
            for layer in range(LAYERS):
                mixer[layer, :K] = fm_proj[layer]
                mixer[layer, K:] = lcb_weight[layer]
                gains[layer] = fm_gain[layer].T
        wanted = min(pieces, (ticks + 1) // 2)
        while issued < wanted:
            exchange(issued)
            issued += 1
        ticks += 1
    while issued < pieces:
        exchange(issued)
        issued += 1

    def step(c, carry):
        here = pl.ds(c * STEP, STEP)
        pltpu.make_async_copy(
            rows.at[pl.ds(0, STEP)], block.at[here, pl.ds(0, 2)], own.at[c]
        ).wait()
        others = block.at[here, pl.ds(0, N - 2)]
        pltpu.make_async_copy(others, others, arrive.at[c]).wait()
        for layer in range(LAYERS):
            features_of_block(
                c * STEP,
                STEP,
                block,
                order if layer == 0 else None,
                full,
                layer,
                mixer,
                gains,
                out_gain,
                inter,
                fm,
            )
        return carry

    lax.fori_loop(0, CHUNKS, step, 0)
    for c in range(CHUNKS):
        here = pl.ds(c * STEP, STEP)
        others = block.at[here, pl.ds(0, N - 2)]
        pltpu.make_async_copy(others, others, send.at[c]).wait()
    for copy in sent:
        copy.wait_send()


def layers(rows, shard, slots, fm_proj, lcb_weight, fm_gain, out_gain):
    vmem = pl.BlockSpec(memory_space=pltpu.VMEM)
    hbm = pl.BlockSpec(memory_space=pl.ANY)
    return pl.pallas_call(
        kernel,
        out_shape=pltpu.VMEM((BLOCK, N, D), BF16),
        in_specs=[hbm, hbm, vmem, vmem, vmem, vmem, vmem],
        out_specs=vmem,
        scratch_shapes=[
            pltpu.VMEM((LAYERS, K, N, 2048), BF16),
            pltpu.VMEM((N, N), BF16),
            pltpu.VMEM((LAYERS, N, N), BF16),
            pltpu.VMEM((LAYERS, K, N), F32),
            pltpu.VMEM((2, STEP * K, D), F32),
            pltpu.VMEM((STEP * K, D), F32),
            pltpu.SemaphoreType.DMA((CHUNKS,)),
            pltpu.SemaphoreType.DMA((CHUNKS,)),
            pltpu.SemaphoreType.DMA((PUSHES,)),
            pltpu.SemaphoreType.DMA((PUSHES,)),
            pltpu.SemaphoreType.DMA((CHUNKS,)),
            pltpu.SemaphoreType.DMA((LAYERS, 2)),
        ],
        compiler_params=pltpu.CompilerParams(
            collective_id=0, has_side_effects=True, vmem_limit_bytes=40 << 20
        ),
    )(rows, shard, slots, fm_proj, lcb_weight, fm_gain, out_gain)


def body(pooled, feature_order, fm_proj, fm_gain, mlp_weight, lcb_weight, out_gain):
    first = lax.rem(lax.axis_index("dp"), 2) * HALF
    slabs = lax.dynamic_slice_in_dim(mlp_weight.reshape(LAYERS, N, K, 256), first, HALF, axis=2)
    shard = slabs.transpose(0, 2, 1, 3)
    gains = fm_gain.reshape(LAYERS, N, K)
    slots = feature_order.reshape(1, N)
    out_gains = out_gain.reshape(LAYERS, 1, D)
    projections = fm_proj.transpose(0, 2, 1)
    return layers(pooled, shard, slots, projections, lcb_weight, gains, out_gains)


def solution(mesh):
    placed = (P(None, ("dp", "fsdp"), None), P(), P(), P(), P(None, None, "fsdp"), P(), P())
    return jax.shard_map(
        body, mesh=mesh, in_specs=placed, out_specs=P(("dp", "fsdp"), None, None), check_vma=False
    )
```
